32 devices in a mesh: cand: 2 (over core), mp: 8 (over z, y), dp: 2 (over x).
Axes of the slice: x: 2, y: 2, z: 4, core: 2. Of those that a mesh axis runs over, the one named last changes fastest.
Arguments:
- clean: bfloat16 [1536, 768], P('mp', 'dp'), may hold values from -3 to 3
- noise: bfloat16 [1536, 768], P('mp', 'dp'), may hold values from -6 to 6
- level_index: int32 [12], P('dp'), may hold values from 0 to 31
- snap_first: bfloat16 [16, 9, 1536, 1536], P('cand', None, 'mp'), may hold values from -0.0546875 to 0.0546875
- snap_second: bfloat16 [16, 9, 1536, 1536], P('cand', None, 'mp'), may hold values from -0.0546875 to 0.0546875
- blend: float32 [4, 8], P('cand'), may hold values from -1.4 to 1.4
- snap_index: int32 [4, 8], P('cand'), may hold values from 0 to 15
Outputs:
- losses: float32 [4], P('cand')
- denoised: bfloat16 [4, 1536, 768], P('cand', 'mp', 'dp')
The draws below stay inside these ranges and needn't reach their ends.
All inputs are finite; a program needn't handle non-finite values.
Results may differ from the reference program's by a relative error of at most 0.00265.
The reference program's roundings to bfloat16 on the way (of `x_in` and `hidden`) count: a program that leaves them out, or rounds other values in their place, can miss the bound.
Values may be sent and summed in bfloat16 or wider, within the bound.
A program may use at most 384 MiB of HBM per device.

```python
import jax
import jax.numpy as jnp
from jax import lax

C = 1536
CANDS = 4
SNAPS = 16
USE = 8
LEVELS = 32
IMAGES = 12
TOKENS = 768


def plant(array, rng, low, largest):
    shape = array.shape
    spot = [jax.random.randint(jax.random.fold_in(rng, axis), (), 0, shape[axis]) for axis in range(len(shape))]
    array = array.at[tuple(spot)].set(low)
    longest = shape.index(max(shape))
    spot[longest] = (spot[longest] + 1) % shape[longest]
    return array.at[tuple(spot)].set(largest)


def levels(own_key, extent, pieces, low, largest):
    factor_of = 1.0
    for position, parts in pieces:
        heights = jax.random.uniform(jax.random.fold_in(jax.random.fold_in(own_key, 6), position), (parts,), jnp.float32, low / len(pieces), largest / len(pieces))
        factor_of = factor_of * jnp.repeat(jnp.exp(heights), extent[position] // parts).reshape((-1,) + (1,) * (len(extent) - 1 - position))
    return factor_of


def scatter_about(key, shape, scale, reach, split=(), dtype=jnp.bfloat16):
    array = scale * jax.random.normal(key, shape, jnp.float32)
    if split:
        array = array * levels(key, shape, split, -0.22, 0.18)
    return jnp.clip(array, -reach, reach).astype(dtype)


def setup_inputs(seed: int = 0) -> dict:
    splits = jax.random.split(jax.random.key(seed), 8)
    return {
        "clean": scatter_about(splits[0], (C, TOKENS), 0.5, 3.0, ((0, 8), (1, 2))),
        "noise": scatter_about(splits[1], (C, TOKENS), 1.0, 6.0, ((0, 8), (1, 2))),
        "level_index": plant(jax.random.randint(splits[2], (IMAGES,), 0, LEVELS), jax.random.fold_in(splits[2], 1), 0, LEVELS - 1).astype(jnp.int32),
        "snap_first": scatter_about(splits[3], (SNAPS, 9, C, C), (9 * C) ** -0.5, 0.0546875, ((0, 2), (2, 8))),
        "snap_second": scatter_about(splits[4], (SNAPS, 9, C, C), (9 * C) ** -0.5, 0.0546875, ((0, 2), (2, 8))),
        "blend": scatter_about(splits[5], (CANDS, USE), 0.35, 1.4, ((0, 2),), jnp.float32),
        "snap_index": plant(jax.random.randint(splits[6], (CANDS, USE), 0, SNAPS), jax.random.fold_in(splits[6], 1), 0, SNAPS - 1).astype(jnp.int32),
    }


SIGMA_DATA = 0.5

def noise_scale(level_index):
    ratio = 2.0 * level_index.astype(jnp.float32) / (LEVELS - 1) - 1.0
    return jnp.exp(-0.4 + 2.0 * ratio)

def tap_shift(values, down_by, right_by):
    length_all = values.shape[-1]
    offset = down_by * 8 + right_by
    padded = jnp.pad(values, [(0, 0)] * (values.ndim - 1) + [(9, 9)])
    moved = lax.slice_in_dim(padded, 9 + offset, 9 + offset + length_all, axis=values.ndim - 1)
    within = jnp.arange(length_all) % 64
    map_row = within // 8
    map_col = within % 8
    inside = (map_row + down_by >= 0) & (map_row + down_by < 8) & (map_col + right_by >= 0) & (map_col + right_by < 8)
    return jnp.where(inside, moved, jnp.zeros_like(moved))

def tap_stack(values):
    return jnp.stack([tap_shift(values, down_by, right_by) for down_by in (-1, 0, 1) for right_by in (-1, 0, 1)], 0)

def reference(clean, noise, level_index, snap_first, snap_second, blend, snap_index):
    sigmas = jnp.repeat(noise_scale(level_index), 64)
    spread = sigmas * sigmas + SIGMA_DATA * SIGMA_DATA
    scale_in = 1.0 / jnp.sqrt(spread)
    scale_skip = SIGMA_DATA * SIGMA_DATA / spread
    scale_out = sigmas * SIGMA_DATA / jnp.sqrt(spread)
    weighting = spread / (sigmas * SIGMA_DATA) ** 2
    clean_f = clean.astype(jnp.float32)
    noisy = clean_f + sigmas * noise.astype(jnp.float32)
    x_in = (scale_in * noisy).astype(jnp.bfloat16)
    x_stack = tap_stack(x_in).astype(jnp.float32)
    width = clean.shape[0]

    def candidate_loss(member):

        def accumulate(which, totals):
            chosen = snap_index[member, which].astype(jnp.int32)
            coeff = blend[member, which]
            first_snap = lax.dynamic_index_in_dim(snap_first, chosen, 0, keepdims=False).astype(jnp.float32)
            second_snap = lax.dynamic_index_in_dim(snap_second, chosen, 0, keepdims=False).astype(jnp.float32)
            return (totals[0] + coeff * first_snap, totals[1] + coeff * second_snap)
        empty = jnp.zeros((9, width, width), jnp.float32)
        first_w, second_w = lax.fori_loop(0, USE, accumulate, (empty, empty))
        first_w = lax.optimization_barrier(first_w.astype(jnp.bfloat16)).astype(jnp.float32)
        second_w = lax.optimization_barrier(second_w.astype(jnp.bfloat16)).astype(jnp.float32)
        preact = jnp.einsum('koc,kct->ot', first_w, x_stack, precision=lax.Precision.HIGHEST)
        hidden = lax.optimization_barrier(jax.nn.silu(preact).astype(jnp.bfloat16))
        h_stack = tap_stack(hidden).astype(jnp.float32)
        feature = jnp.einsum('kio,kit->ot', second_w, h_stack, precision=lax.Precision.HIGHEST)
        denoised_f = scale_skip * noisy + scale_out * feature
        loss_value = jnp.mean(weighting * (denoised_f - clean_f) ** 2)
        return (loss_value, denoised_f.astype(jnp.bfloat16))
    losses, denoised = lax.map(candidate_loss, jnp.arange(CANDS))
    return (losses, denoised)
```

```python
import functools

import jax
import jax.numpy as jnp
from jax import lax
from jax.experimental import pallas as pl
from jax.experimental.pallas import tpu as pltpu
from jax.sharding import PartitionSpec as P

LEVELS = 32
SIGMA_DATA = 0.5
MESH = pl.DeviceIdType.MESH


def from_partner(value, axis, apart):
    return lax.ppermute(value, axis, [(i, i ^ 1 << apart) for i in range(lax.axis_size(axis))])


def noise_scale(level_index):
    ratio = 2.0 * level_index.astype(jnp.float32) / (LEVELS - 1) - 1.0
    return jnp.exp(-0.4 + 2.0 * ratio)


def tap_matrix(tap):
    down_by, right_by = tap // 3 - 1, tap % 3 - 1
    source = lax.broadcasted_iota(jnp.int32, (128, 128), 0)
    target = lax.broadcasted_iota(jnp.int32, (128, 128), 1)
    row, col = (target & 63) >> 3, target & 7
    inside = (
        (row + down_by >= 0) & (row + down_by < 8) & (col + right_by >= 0) & (col + right_by < 8)
    )
    hit = (source == target + (down_by * 8 + right_by)) & inside
    return jnp.where(hit, 1.0, 0.0).astype(jnp.bfloat16)


def conv_kernel(
    taps, groups, mix_ref, x_ref, first_ref, second_ref, out_ref,
    give, mine, got, x_full, x_tap, pre, hidden,
    send_sem, recv_sem, x_send, x_recv,
):
    step = pl.program_id(0)
    chunks = 2 * taps
    snaps, rows, width = first_ref.shape[0], first_ref.shape[2], first_ref.shape[3]
    members, tokens = pre.shape[0], pre.shape[2]
    tiles = tokens // 128
    cand, me = lax.axis_index("cand"), lax.axis_index("mp")
    partner = 1 - cand
    block = 16 if rows % 16 == 0 else rows

    def exchange(chunk):
        return pltpu.make_async_remote_copy(
            src_ref=give.at[chunk % 2],
            dst_ref=got.at[chunk % 4],
            send_sem=send_sem.at[chunk % 2],
            recv_sem=recv_sem.at[chunk % 4],
            device_id={"cand": partner},
            device_id_type=MESH,
        )

    def x_copy(away, slot):
        return pltpu.make_async_remote_copy(
            src_ref=x_ref,
            dst_ref=x_full.at[slot],
            send_sem=x_send.at[away],
            recv_sem=x_recv.at[away],
            device_id={"mp": (me + away) % groups},
            device_id_type=MESH,
        )

    @pl.when(step == 0)
    def _():
        barrier = pltpu.get_barrier_semaphore()
        pl.semaphore_signal(barrier, inc=1, device_id={"cand": partner}, device_id_type=MESH)
        for away in range(1, groups):
            pl.semaphore_signal(
                barrier, inc=1, device_id={"mp": (me + away) % groups}, device_id_type=MESH
            )
        pl.semaphore_wait(barrier, groups)
        for away in range(1, groups):
            x_copy(away, me).start()
        x_full[me] = x_ref[...]
        pre[...] = jnp.zeros_like(pre)
        out_ref[...] = jnp.zeros_like(out_ref)

    def blend(source):
        coeff = [[mix_ref[c, s] for s in range(snaps)] for c in range(2 * members)]
        slot = step % 2

        def body(which, carry):
            at = pl.ds(pl.multiple_of(which * block, block), block)
            for tile in range(width // 128):
                lanes = pl.ds(tile * 128, 128)
                totals = [None] * (2 * members)
                for s in range(snaps):
                    value = source[s, 0, at, lanes].astype(jnp.float32)
                    for c in range(2 * members):
                        term = coeff[c][s] * value
                        totals[c] = term if s == 0 else totals[c] + term
                for c in range(members):
                    mine[slot, c, at, lanes] = totals[c]
                    give[slot, c, at, lanes] = totals[members + c]
            return carry

        lax.fori_loop(0, rows // block, body, 0)

    @pl.when((step >= 2) & (step < chunks))
    def _():
        exchange(step - 2).wait_send()

    @pl.when(step < taps)
    def _():
        blend(first_ref)

    @pl.when((step >= taps) & (step < chunks))
    def _():
        blend(second_ref)

    @pl.when(step < chunks)
    def _():
        exchange(step).start()

    @pl.when(step == 1)
    def _():
        for away in range(1, groups):
            copy = x_copy(away, (me + groups - away) % groups)
            copy.wait_send()
            copy.wait_recv()

    done = step - 1

    @pl.when(step >= 1)
    def _():
        exchange(done).wait_recv()

    @pl.when((step >= 1) & (done < taps))
    def _():
        shift = tap_matrix(done)
        for group in range(groups):
            for tile in range(tiles):
                lanes = pl.ds(tile * 128, 128)
                x_tap[pl.ds(group * rows, rows), lanes] = jnp.dot(
                    x_full[group, :, lanes], shift, preferred_element_type=jnp.float32
                ).astype(jnp.bfloat16)
        for c in range(members):
            weight = (mine[done % 2, c] + got[done % 4, c]).astype(jnp.bfloat16)
            pre[c] += jnp.dot(weight, x_tap[...], preferred_element_type=jnp.float32)

    @pl.when(done == taps - 1)
    def _():
        value = pre[...]
        hidden[...] = (value * jax.nn.sigmoid(value)).astype(jnp.bfloat16)

    @pl.when((step >= 1) & (done >= taps))
    def _():
        shift = tap_matrix(done - taps)
        for c in range(members):
            shifted = jnp.concatenate(
                [
                    jnp.dot(
                        hidden[c, :, pl.ds(tile * 128, 128)],
                        shift,
                        preferred_element_type=jnp.float32,
                    ).astype(jnp.bfloat16)
                    for tile in range(tiles)
                ],
                axis=1,
            )
            for part in range(width // 256):
                lanes = pl.ds(part * 256, 256)
                weight = (mine[done % 2, c, :, lanes] + got[done % 4, c, :, lanes]).astype(
                    jnp.bfloat16
                )
                out_ref[lanes, pl.ds(c * tokens, tokens)] += lax.dot_general(
                    weight, shifted, (((0,), (0,)), ((), ())), preferred_element_type=jnp.float32
                )

    @pl.when(step == chunks)
    def _():
        exchange(chunks - 2).wait_send()
        exchange(chunks - 1).wait_send()


def convolve(mix, x_own, snap_first, snap_second, groups):
    snaps, taps, rows, width = snap_first.shape
    members, tokens = mix.shape[0] // 2, x_own.shape[1]
    pair = (members, rows, width)
    return pl.pallas_call(
        functools.partial(conv_kernel, taps, groups),
        grid=(2 * taps + 1,),
        out_shape=jax.ShapeDtypeStruct((width, members * tokens), jnp.float32),
        in_specs=[
            pl.BlockSpec(memory_space=pltpu.SMEM),
            pl.BlockSpec((rows, tokens), lambda i: (0, 0)),
            pl.BlockSpec((snaps, 1, rows, width), lambda i: (0, jnp.minimum(i, taps - 1), 0, 0)),
            pl.BlockSpec(
                (snaps, 1, rows, width), lambda i: (0, jnp.clip(i - taps, 0, taps - 1), 0, 0)
            ),
        ],
        out_specs=pl.BlockSpec((width, members * tokens), lambda i: (0, 0)),
        scratch_shapes=[
            pltpu.VMEM((2,) + pair, jnp.float32),
            pltpu.VMEM((2,) + pair, jnp.float32),
            pltpu.VMEM((4,) + pair, jnp.float32),
            pltpu.VMEM((groups, rows, tokens), jnp.bfloat16),
            pltpu.VMEM((width, tokens), jnp.bfloat16),
            pltpu.VMEM((members, rows, tokens), jnp.float32),
            pltpu.VMEM((members, rows, tokens), jnp.bfloat16),
            pltpu.SemaphoreType.DMA((2,)),
            pltpu.SemaphoreType.DMA((4,)),
            pltpu.SemaphoreType.DMA((groups,)),
            pltpu.SemaphoreType.DMA((groups,)),
        ],
        compiler_params=pltpu.CompilerParams(
            collective_id=0,
            has_side_effects=True,
            dimension_semantics=("arbitrary",),
            vmem_limit_bytes=64 * 1024 * 1024 - 65536,
        ),
        name="blend_convolve",
    )(mix, x_own, snap_first, snap_second)


def total_kernel(groups, images, own_ref, out_ref, held, send_sem, recv_sem):
    me = lax.axis_index("mp") * images + lax.axis_index("dp")
    peers = groups * images

    def copy(away):
        to = (me + away) % peers
        return pltpu.make_async_remote_copy(
            src_ref=own_ref,
            dst_ref=held.at[away],
            send_sem=send_sem.at[away],
            recv_sem=recv_sem.at[away],
            device_id={"mp": to // images, "dp": to % images},
            device_id_type=MESH,
        )

    barrier = pltpu.get_barrier_semaphore()
    for away in range(1, peers):
        to = (me + away) % peers
        pl.semaphore_signal(
            barrier,
            inc=1,
            device_id={"mp": to // images, "dp": to % images},
            device_id_type=MESH,
        )
    pl.semaphore_wait(barrier, peers - 1)
    for away in range(1, peers):
        copy(away).start()
    total = own_ref[...]
    for away in range(1, peers):
        copy(away).wait_recv()
        total = total + held[away]
    out_ref[...] = total
    for away in range(1, peers):
        copy(away).wait_send()


def total_over(partial, groups, images):
    peers = groups * images
    return pl.pallas_call(
        functools.partial(total_kernel, groups, images),
        out_shape=jax.ShapeDtypeStruct(partial.shape, jnp.float32),
        in_specs=[pl.BlockSpec(memory_space=pltpu.VMEM)],
        out_specs=pl.BlockSpec(memory_space=pltpu.VMEM),
        scratch_shapes=[
            pltpu.VMEM((peers,) + partial.shape, jnp.float32),
            pltpu.SemaphoreType.DMA((peers,)),
            pltpu.SemaphoreType.DMA((peers,)),
        ],
        compiler_params=pltpu.CompilerParams(collective_id=1, has_side_effects=True),
        name="loss_total",
    )(partial)


def on_device(clean, noise, level_index, snap_first, snap_second, blend, snap_index):
    sigmas = jnp.repeat(noise_scale(level_index), 64)
    spread = sigmas * sigmas + SIGMA_DATA * SIGMA_DATA
    scale_in = 1.0 / jnp.sqrt(spread)
    scale_skip = SIGMA_DATA * SIGMA_DATA / spread
    scale_out = sigmas * SIGMA_DATA / jnp.sqrt(spread)
    weighting = spread / (sigmas * SIGMA_DATA) ** 2
    clean_f = clean.astype(jnp.float32)
    noisy = clean_f + sigmas * noise.astype(jnp.float32)
    x_own = (scale_in * noisy).astype(jnp.bfloat16)
    owned = snap_first.shape[0]
    stored = owned * lax.axis_size("cand")
    groups, images = lax.axis_size("mp"), lax.axis_size("dp")
    onehot = (snap_index[:, :, None] == jnp.arange(stored, dtype=jnp.int32)[None, None, :]).astype(
        jnp.float32
    )
    mixing = jnp.sum(blend[:, :, None] * onehot, 1)
    other_mix = from_partner(mixing, "cand", 0)
    first_slot = lax.axis_index("cand") * owned
    mix = lax.dynamic_slice_in_dim(jnp.concatenate([mixing, other_mix], 0), first_slot, owned, 1)
    members = blend.shape[0]
    sums = convolve(mix, x_own, snap_first, snap_second, groups)
    feature = lax.psum_scatter(sums, "mp", scatter_dimension=0, tiled=True)
    tokens = clean.shape[1]
    features = jnp.stack([feature[:, c * tokens : (c + 1) * tokens] for c in range(members)], 0)
    denoised_f = scale_skip[None, None, :] * noisy[None] + scale_out[None, None, :] * features
    partial_value = jnp.sum(
        weighting[None, None, :] * (denoised_f - clean_f[None]) ** 2, axis=(1, 2)
    )
    entries = clean.shape[0] * groups * clean.shape[1] * images
    tile = jnp.broadcast_to(jnp.pad(partial_value, (0, 8 - members))[:, None], (8, 128))
    losses = total_over(tile, groups, images)[:members, 0] / entries
    return (losses, denoised_f.astype(jnp.bfloat16))


def solution(mesh):
    placed = (
        P("mp", "dp"),
        P("mp", "dp"),
        P("dp"),
        P("cand", None, "mp", None),
        P("cand", None, "mp", None),
        P("cand", None),
        P("cand", None),
    )
    return jax.shard_map(
        on_device,
        mesh=mesh,
        in_specs=placed,
        out_specs=(P("cand"), P("cand", "mp", "dp")),
        check_vma=False,
    )
```

```python
import functools
import math

import jax
import jax.numpy as jnp
from jax import lax
from jax.experimental import pallas as pl
from jax.experimental.pallas import tpu as pltpu
from jax.sharding import PartitionSpec as P

LEVELS = 32
SIGMA_DATA = 0.5
MESH = pl.DeviceIdType.MESH


def from_partner(value, axis, apart):
    return lax.ppermute(value, axis, [(i, i ^ 1 << apart) for i in range(lax.axis_size(axis))])


def noise_scale(level_index):
    ratio = 2.0 * level_index.astype(jnp.float32) / (LEVELS - 1) - 1.0
    return jnp.exp(-0.4 + 2.0 * ratio)


def tap_matrix(tap):
    down_by, right_by = tap // 3 - 1, tap % 3 - 1
    source = lax.broadcasted_iota(jnp.int32, (128, 128), 0)
    target = lax.broadcasted_iota(jnp.int32, (128, 128), 1)
    row, col = (target & 63) >> 3, target & 7
    inside = (
        (row + down_by >= 0) & (row + down_by < 8) & (col + right_by >= 0) & (col + right_by < 8)
    )
    hit = (source == target + (down_by * 8 + right_by)) & inside
    return jnp.where(hit, 1.0, 0.0).astype(jnp.bfloat16)


def conv_kernel(
    taps, groups, span, few, mix_ref, x_ref, first_ref, second_ref, out_ref,
    give, mine, got, x_full, x_tap, pre, hidden, sums, paired, landed,
    send_sem, recv_sem, x_send, x_recv, pair_send, pair_recv, owner_send, owner_recv,
):
    step = pl.program_id(0)
    snaps, rows, width = first_ref.shape[0], first_ref.shape[2], first_ref.shape[3]
    members, tokens = pre.shape[0], pre.shape[2]
    tiles = tokens // 128
    pieces, parts = width // span, taps // few
    chunks = taps + pieces * parts
    pairs, couples = groups // 2, span // (2 * rows)
    cand, me = lax.axis_index("cand"), lax.axis_index("mp")
    partner = 1 - cand
    side = me % 2
    my_piece = me // (2 * couples)
    block = 16 if rows % 16 == 0 else rows

    def exchange(chunk, count):
        return pltpu.make_async_remote_copy(
            src_ref=give.at[chunk % 2, :, pl.ds(0, count)],
            dst_ref=got.at[chunk % 4, :, pl.ds(0, count)],
            send_sem=send_sem.at[chunk % 2],
            recv_sem=recv_sem.at[chunk % 4],
            device_id={"cand": partner},
            device_id_type=MESH,
        )

    def x_copy(away, slot):
        return pltpu.make_async_remote_copy(
            src_ref=x_ref,
            dst_ref=x_full.at[slot],
            send_sem=x_send.at[away],
            recv_sem=x_recv.at[away],
            device_id={"mp": (me + away) % groups},
            device_id_type=MESH,
        )

    def piece_of(stage):
        return (my_piece + stage + 1) % pieces

    def pair_copy(couple):
        return pltpu.make_async_remote_copy(
            src_ref=sums.at[2 * couple + 1 - side],
            dst_ref=paired.at[couple],
            send_sem=pair_send.at[couple],
            recv_sem=pair_recv.at[couple],
            device_id={"mp": me + 1 - 2 * side},
            device_id_type=MESH,
        )

    def owner_copy(couple, slot):
        return pltpu.make_async_remote_copy(
            src_ref=paired.at[couple],
            dst_ref=landed.at[slot],
            send_sem=owner_send.at[couple],
            recv_sem=owner_recv.at[slot],
            device_id={"mp": 2 * couple + side},
            device_id_type=MESH,
        )

    def start_pairs(stage):
        for which in range(couples):
            pair_copy(piece_of(stage) * couples + which).start()

    def finish_pairs(stage):
        for which in range(couples):
            couple = piece_of(stage) * couples + which
            pair_copy(couple).wait_recv()
            paired[couple] = paired[couple] + sums[2 * couple + side]

            @pl.when(couple != me // 2)
            def _():
                owner_copy(couple, me // 2).start()

    @pl.when(step == 0)
    def _():
        barrier = pltpu.get_barrier_semaphore()
        pl.semaphore_signal(barrier, inc=1, device_id={"cand": partner}, device_id_type=MESH)
        for away in range(1, groups):
            pl.semaphore_signal(
                barrier, inc=1, device_id={"mp": (me + away) % groups}, device_id_type=MESH
            )
        pl.semaphore_wait(barrier, groups)
        for away in range(1, groups):
            x_copy(away, me).start()
        x_full[me] = x_ref[...]
        pre[...] = jnp.zeros_like(pre)

    def blend(source, count, columns, place):
        coeff = [[mix_ref[c, s] for s in range(snaps)] for c in range(2 * members)]
        slot = step % 2

        def body(which, carry):
            at = pl.ds(pl.multiple_of(which * block, block), block)
            for tap in range(count):
                for tile in range(columns // 128):
                    lanes = pl.ds(tile * 128, 128)
                    totals = [None] * (2 * members)
                    for s in range(snaps):
                        value = source[s, tap, at, lanes].astype(jnp.float32)
                        for c in range(2 * members):
                            term = coeff[c][s] * value
                            totals[c] = term if s == 0 else totals[c] + term
                    piece, first = place(tap, tile)
                    for c in range(members):
                        mine[slot, c, piece, at, pl.ds(first, 128)] = totals[c]
                        give[slot, c, piece, at, pl.ds(first, 128)] = totals[members + c]
            return carry

        lax.fori_loop(0, rows // block, body, 0)

    @pl.when((step >= 2) & (step < taps + 2))
    def _():
        exchange(step - 2, pieces).wait_send()

    @pl.when((step >= taps + 2) & (step < chunks))
    def _():
        exchange(step - 2, few).wait_send()

    @pl.when(step < taps)
    def _():
        blend(first_ref, 1, width, lambda tap, tile: (tile * 128 // span, tile * 128 % span))
        exchange(step, pieces).start()

    @pl.when((step >= taps) & (step < chunks))
    def _():
        blend(second_ref, few, span, lambda tap, tile: (tap, tile * 128))
        exchange(step, few).start()

    @pl.when(step == 1)
    def _():
        for away in range(1, groups):
            copy = x_copy(away, (me + groups - away) % groups)
            copy.wait_send()
            copy.wait_recv()

    done = step - 1

    def weight_of(c, piece):
        return (mine[done % 2, c, piece] + got[done % 4, c, piece]).astype(jnp.bfloat16)

    @pl.when((step >= 1) & (done < taps))
    def _():
        shift = tap_matrix(done)
        for group in range(groups):
            for tile in range(tiles):
                lanes = pl.ds(tile * 128, 128)
                x_tap[pl.ds(group * rows, rows), lanes] = jnp.dot(
                    x_full[group, :, lanes], shift, preferred_element_type=jnp.float32
                ).astype(jnp.bfloat16)
        exchange(done, pieces).wait_recv()
        for c in range(members):
            weight = jnp.concatenate([weight_of(c, piece) for piece in range(pieces)], axis=1)
            pre[c] += jnp.dot(weight, x_tap[...], preferred_element_type=jnp.float32)

    @pl.when(done == taps - 1)
    def _():
        value = pre[...]
        hidden[...] = (value * jax.nn.sigmoid(value)).astype(jnp.bfloat16)

    @pl.when((step >= 1) & (done >= taps))
    def _():
        at = done - taps
        stage, part = at // parts, at % parts
        owners = piece_of(stage) * 2 * couples
        shifts = [tap_matrix(part * few + tap) for tap in range(few)]
        exchange(done, few).wait_recv()
        for c in range(members):
            moved = [
                jnp.concatenate(
                    [
                        jnp.dot(
                            hidden[c, :, pl.ds(tile * 128, 128)],
                            shift,
                            preferred_element_type=jnp.float32,
                        ).astype(jnp.bfloat16)
                        for tile in range(tiles)
                    ],
                    axis=1,
                )
                for shift in shifts
            ]
            weight = jnp.concatenate([weight_of(c, tap) for tap in range(few)], axis=0)
            product = lax.dot_general(
                weight,
                jnp.concatenate(moved, axis=0),
                (((0,), (0,)), ((), ())),
                preferred_element_type=jnp.float32,
            )
            lanes = pl.ds(c * tokens, tokens)

            @pl.when(part == 0)
            def _():
                for which in range(2 * couples):
                    sums[owners + which, :, lanes] = product[which * rows : (which + 1) * rows]

            @pl.when(part > 0)
            def _():
                for which in range(2 * couples):
                    sums[owners + which, :, lanes] += product[which * rows : (which + 1) * rows]

        @pl.when(part == parts - 1)
        def _():
            start_pairs(stage)

            @pl.when(stage >= 1)
            def _():
                finish_pairs(stage - 1)

    @pl.when(step == chunks)
    def _():
        finish_pairs(pieces - 1)
        total = paired[me // 2]
        for away in range(1, pairs):
            source = (me // 2 + pairs - away) % pairs
            owner_copy((me // 2 + away) % pairs, source).wait_recv()
            total = total + landed[source]
        out_ref[...] = total
        for away in range(1, pairs):
            owner_copy((me // 2 + away) % pairs, me // 2).wait_send()
        for couple in range(pairs):
            pair_copy(couple).wait_send()
        exchange(chunks - 2, few).wait_send()
        exchange(chunks - 1, few).wait_send()


def convolve(mix, x_own, snap_first, snap_second, groups):
    snaps, taps, rows, width = snap_first.shape
    members, tokens = mix.shape[0] // 2, x_own.shape[1]
    span = math.lcm(128, 2 * rows)
    few = 3
    pieces, parts = width // span, taps // few
    couples, pairs = span // (2 * rows), groups // 2
    part = (members, max(pieces, few), rows, span)
    sums = (rows, members * tokens)

    def second_block(i):
        at = jnp.clip(i - taps, 0, pieces * parts - 1)
        piece = (lax.axis_index("mp") // (2 * couples) + at // parts + 1) % pieces
        return 0, at % parts, 0, piece

    return pl.pallas_call(
        functools.partial(conv_kernel, taps, groups, span, few),
        grid=(taps + pieces * parts + 1,),
        out_shape=jax.ShapeDtypeStruct(sums, jnp.float32),
        in_specs=[
            pl.BlockSpec(memory_space=pltpu.SMEM),
            pl.BlockSpec((rows, tokens), lambda i: (0, 0)),
            pl.BlockSpec((snaps, 1, rows, width), lambda i: (0, jnp.minimum(i, taps - 1), 0, 0)),
            pl.BlockSpec((snaps, few, rows, span), second_block),
        ],
        out_specs=pl.BlockSpec(sums, lambda i: (0, 0)),
        scratch_shapes=[
            pltpu.VMEM((2,) + part, jnp.float32),
            pltpu.VMEM((2,) + part, jnp.float32),
            pltpu.VMEM((4,) + part, jnp.float32),
            pltpu.VMEM((groups, rows, tokens), jnp.bfloat16),
            pltpu.VMEM((width, tokens), jnp.bfloat16),
            pltpu.VMEM((members, rows, tokens), jnp.float32),
            pltpu.VMEM((members, rows, tokens), jnp.bfloat16),
            pltpu.VMEM((groups,) + sums, jnp.float32),
            pltpu.VMEM((pairs,) + sums, jnp.float32),
            pltpu.VMEM((pairs,) + sums, jnp.float32),
            pltpu.SemaphoreType.DMA((2,)),
            pltpu.SemaphoreType.DMA((4,)),
            pltpu.SemaphoreType.DMA((groups,)),
            pltpu.SemaphoreType.DMA((groups,)),
            pltpu.SemaphoreType.DMA((pairs,)),
            pltpu.SemaphoreType.DMA((pairs,)),
            pltpu.SemaphoreType.DMA((pairs,)),
            pltpu.SemaphoreType.DMA((pairs,)),
        ],
        compiler_params=pltpu.CompilerParams(
            collective_id=0,
            has_side_effects=True,
            dimension_semantics=("arbitrary",),
            vmem_limit_bytes=64 * 1024 * 1024 - 65536,
        ),
        name="blend_convolve",
    )(mix, x_own, snap_first, snap_second)


def total_kernel(groups, images, own_ref, out_ref, held, send_sem, recv_sem):
    me = lax.axis_index("mp") * images + lax.axis_index("dp")
    peers = groups * images

    def copy(away):
        to = (me + away) % peers
        return pltpu.make_async_remote_copy(
            src_ref=own_ref,
            dst_ref=held.at[away],
            send_sem=send_sem.at[away],
            recv_sem=recv_sem.at[away],
            device_id={"mp": to // images, "dp": to % images},
            device_id_type=MESH,
        )

    barrier = pltpu.get_barrier_semaphore()
    for away in range(1, peers):
        to = (me + away) % peers
        pl.semaphore_signal(
            barrier,
            inc=1,
            device_id={"mp": to // images, "dp": to % images},
            device_id_type=MESH,
        )
    pl.semaphore_wait(barrier, peers - 1)
    for away in range(1, peers):
        copy(away).start()
    total = own_ref[...]
    for away in range(1, peers):
        copy(away).wait_recv()
        total = total + held[away]
    out_ref[...] = total
    for away in range(1, peers):
        copy(away).wait_send()


def total_over(partial, groups, images):
    peers = groups * images
    return pl.pallas_call(
        functools.partial(total_kernel, groups, images),
        out_shape=jax.ShapeDtypeStruct(partial.shape, jnp.float32),
        in_specs=[pl.BlockSpec(memory_space=pltpu.VMEM)],
        out_specs=pl.BlockSpec(memory_space=pltpu.VMEM),
        scratch_shapes=[
            pltpu.VMEM((peers,) + partial.shape, jnp.float32),
            pltpu.SemaphoreType.DMA((peers,)),
            pltpu.SemaphoreType.DMA((peers,)),
        ],
        compiler_params=pltpu.CompilerParams(collective_id=1, has_side_effects=True),
        name="loss_total",
    )(partial)


def on_device(clean, noise, level_index, snap_first, snap_second, blend, snap_index):
    sigmas = jnp.repeat(noise_scale(level_index), 64)
    spread = sigmas * sigmas + SIGMA_DATA * SIGMA_DATA
    scale_in = 1.0 / jnp.sqrt(spread)
    scale_skip = SIGMA_DATA * SIGMA_DATA / spread
    scale_out = sigmas * SIGMA_DATA / jnp.sqrt(spread)
    weighting = spread / (sigmas * SIGMA_DATA) ** 2
    clean_f = clean.astype(jnp.float32)
    noisy = clean_f + sigmas * noise.astype(jnp.float32)
    x_own = (scale_in * noisy).astype(jnp.bfloat16)
    owned = snap_first.shape[0]
    stored = owned * lax.axis_size("cand")
    groups, images = lax.axis_size("mp"), lax.axis_size("dp")
    onehot = (snap_index[:, :, None] == jnp.arange(stored, dtype=jnp.int32)[None, None, :]).astype(
        jnp.float32
    )
    mixing = jnp.sum(blend[:, :, None] * onehot, 1)
    other_mix = from_partner(mixing, "cand", 0)
    first_slot = lax.axis_index("cand") * owned
    mix = lax.dynamic_slice_in_dim(jnp.concatenate([mixing, other_mix], 0), first_slot, owned, 1)
    members = blend.shape[0]
    feature = convolve(mix, x_own, snap_first, snap_second, groups)
    tokens = clean.shape[1]
    features = jnp.stack([feature[:, c * tokens : (c + 1) * tokens] for c in range(members)], 0)
    denoised_f = scale_skip[None, None, :] * noisy[None] + scale_out[None, None, :] * features
    partial_value = jnp.sum(
        weighting[None, None, :] * (denoised_f - clean_f[None]) ** 2, axis=(1, 2)
    )
    entries = clean.shape[0] * groups * clean.shape[1] * images
    tile = jnp.broadcast_to(jnp.pad(partial_value, (0, 8 - members))[:, None], (8, 128))
    losses = total_over(tile, groups, images)[:members, 0] / entries
    return (losses, denoised_f.astype(jnp.bfloat16))


def solution(mesh):
    placed = (
        P("mp", "dp"),
        P("mp", "dp"),
        P("dp"),
        P("cand", None, "mp", None),
        P("cand", None, "mp", None),
        P("cand", None),
        P("cand", None),
    )
    return jax.shard_map(
        on_device,
        mesh=mesh,
        in_specs=placed,
        out_specs=(P("cand"), P("cand", "mp", "dp")),
        check_vma=False,
    )
```

```python
import functools
import math

import jax
import jax.numpy as jnp
from jax import lax
from jax.experimental import pallas as pl
from jax.experimental.pallas import tpu as pltpu
from jax.sharding import PartitionSpec as P

LEVELS = 32
SIGMA_DATA = 0.5
MESH = pl.DeviceIdType.MESH


def from_partner(value, axis, apart):
    return lax.ppermute(value, axis, [(i, i ^ 1 << apart) for i in range(lax.axis_size(axis))])


def noise_scale(level_index):
    ratio = 2.0 * level_index.astype(jnp.float32) / (LEVELS - 1) - 1.0
    return jnp.exp(-0.4 + 2.0 * ratio)


def tap_matrix(tap):
    down_by, right_by = tap // 3 - 1, tap % 3 - 1
    source = lax.broadcasted_iota(jnp.int32, (128, 128), 0)
    target = lax.broadcasted_iota(jnp.int32, (128, 128), 1)
    row, col = (target & 63) >> 3, target & 7
    inside = (
        (row + down_by >= 0) & (row + down_by < 8) & (col + right_by >= 0) & (col + right_by < 8)
    )
    hit = (source == target + (down_by * 8 + right_by)) & inside
    return jnp.where(hit, 1.0, 0.0).astype(jnp.bfloat16)


def conv_kernel(
    taps, groups, span, few, members, mix_ref, x_ref, first_ref, second_ref, out_ref,
    give, mine, got, x_full, x_tap, pre, hidden, sums, paired, landed,
    send_sem, recv_sem, x_send, x_recv, pair_send, pair_recv, owner_send, owner_recv,
):
    step = pl.program_id(0)
    snaps, rows, width = first_ref.shape[0], first_ref.shape[2], first_ref.shape[3]
    tokens = pre.shape[1]
    tiles = tokens // 128
    pieces, parts = width // span, taps // few
    per = taps + pieces * parts
    chunks = members * per
    member, local = step // per, step % per
    pairs, couples = groups // 2, span // (2 * rows)
    cand, me = lax.axis_index("cand"), lax.axis_index("mp")
    partner = 1 - cand
    side = me % 2
    my_piece = me // (2 * couples)
    block = 16 if rows % 16 == 0 else rows

    def exchange(chunk, count):
        return pltpu.make_async_remote_copy(
            src_ref=give.at[chunk % 2, pl.ds(0, count)],
            dst_ref=got.at[chunk % 4, pl.ds(0, count)],
            send_sem=send_sem.at[chunk % 2],
            recv_sem=recv_sem.at[chunk % 4],
            device_id={"cand": partner},
            device_id_type=MESH,
        )

    def x_copy(away, slot):
        return pltpu.make_async_remote_copy(
            src_ref=x_ref,
            dst_ref=x_full.at[slot],
            send_sem=x_send.at[away],
            recv_sem=x_recv.at[away],
            device_id={"mp": (me + away) % groups},
            device_id_type=MESH,
        )

    def piece_of(stage):
        return (my_piece + stage + 1) % pieces

    def pair_copy(which, couple):
        return pltpu.make_async_remote_copy(
            src_ref=sums.at[which * groups + 2 * couple + 1 - side],
            dst_ref=paired.at[which * pairs + couple],
            send_sem=pair_send.at[which * pairs + couple],
            recv_sem=pair_recv.at[which * pairs + couple],
            device_id={"mp": me + 1 - 2 * side},
            device_id_type=MESH,
        )

    def owner_copy(which, couple, slot):
        return pltpu.make_async_remote_copy(
            src_ref=paired.at[which * pairs + couple],
            dst_ref=landed.at[which * pairs + slot],
            send_sem=owner_send.at[which * pairs + couple],
            recv_sem=owner_recv.at[which * pairs + slot],
            device_id={"mp": 2 * couple + side},
            device_id_type=MESH,
        )

    def start_pairs(stage):
        for index in range(couples):
            pair_copy(stage // pieces, piece_of(stage % pieces) * couples + index).start()

    def finish_pairs(stage):
        which = stage // pieces
        for index in range(couples):
            couple = piece_of(stage % pieces) * couples + index
            pair_copy(which, couple).wait_recv()
            at = which * pairs + couple
            paired[at] = paired[at] + sums[which * groups + 2 * couple + side]

            @pl.when(couple != me // 2)
            def _():
                owner_copy(which, couple, me // 2).start()

    @pl.when(step == 0)
    def _():
        barrier = pltpu.get_barrier_semaphore()
        pl.semaphore_signal(barrier, inc=1, device_id={"cand": partner}, device_id_type=MESH)
        for away in range(1, groups):
            pl.semaphore_signal(
                barrier, inc=1, device_id={"mp": (me + away) % groups}, device_id_type=MESH
            )
        pl.semaphore_wait(barrier, groups)
        for away in range(1, groups):
            x_copy(away, me).start()
        x_full[me] = x_ref[...]

    def blend(source, count, columns, place):
        coeff = [[mix_ref[c + member, s] for s in range(snaps)] for c in (0, members)]
        slot = step % 2

        def body(which, carry):
            at = pl.ds(pl.multiple_of(which * block, block), block)
            for tap in range(count):
                for tile in range(columns // 128):
                    lanes = pl.ds(tile * 128, 128)
                    totals = [None, None]
                    for s in range(snaps):
                        value = source[s, tap, at, lanes].astype(jnp.float32)
                        for c in range(2):
                            term = coeff[c][s] * value
                            totals[c] = term if s == 0 else totals[c] + term
                    piece, first = place(tap, tile)
                    mine[slot, piece, at, pl.ds(first, 128)] = totals[0]
                    give[slot, piece, at, pl.ds(first, 128)] = totals[1]
            return carry

        lax.fori_loop(0, rows // block, body, 0)

    earlier = (step + per - 2) % per

    @pl.when((step >= 2) & (step < chunks) & (earlier < taps))
    def _():
        exchange(step - 2, pieces).wait_send()

    @pl.when((step >= 2) & (step < chunks) & (earlier >= taps))
    def _():
        exchange(step - 2, few).wait_send()

    @pl.when((step < chunks) & (local < taps))
    def _():
        blend(first_ref, 1, width, lambda tap, tile: (tile * 128 // span, tile * 128 % span))
        exchange(step, pieces).start()

    @pl.when((step < chunks) & (local >= taps))
    def _():
        blend(second_ref, few, span, lambda tap, tile: (tap, tile * 128))
        exchange(step, few).start()

    @pl.when(step == 1)
    def _():
        for away in range(1, groups):
            copy = x_copy(away, (me + groups - away) % groups)
            copy.wait_send()
            copy.wait_recv()

    done = step - 1
    past = (step + per - 1) % per

    def weight_of(piece):
        return (mine[done % 2, piece] + got[done % 4, piece]).astype(jnp.bfloat16)

    @pl.when((step >= 1) & (done < taps))
    def _():
        shift = tap_matrix(past)
        for group in range(groups):
            for tile in range(tiles):
                lanes = pl.ds(tile * 128, 128)
                x_tap[past, pl.ds(group * rows, rows), lanes] = jnp.dot(
                    x_full[group, :, lanes], shift, preferred_element_type=jnp.float32
                ).astype(jnp.bfloat16)

    @pl.when((step >= 1) & (past < taps))
    def _():
        exchange(done, pieces).wait_recv()
        weight = jnp.concatenate([weight_of(piece) for piece in range(pieces)], axis=1)
        product = jnp.dot(weight, x_tap[past], preferred_element_type=jnp.float32)

        @pl.when(past == 0)
        def _():
            pre[...] = product

        @pl.when(past > 0)
        def _():
            pre[...] += product

    @pl.when((step >= 1) & (past == taps - 1))
    def _():
        value = pre[...]
        hidden[...] = (value * jax.nn.sigmoid(value)).astype(jnp.bfloat16)

    @pl.when((step >= 1) & (past >= taps))
    def _():
        stage, part = (past - taps) // parts, (past - taps) % parts
        which = done // per
        owners = which * groups + piece_of(stage) * 2 * couples
        exchange(done, few).wait_recv()
        moved = []
        for tap in range(few):
            shift = tap_matrix(part * few + tap)
            moved.append(
                jnp.concatenate(
                    [
                        jnp.dot(
                            hidden[:, pl.ds(tile * 128, 128)],
                            shift,
                            preferred_element_type=jnp.float32,
                        ).astype(jnp.bfloat16)
                        for tile in range(tiles)
                    ],
                    axis=1,
                )
            )
        product = lax.dot_general(
            jnp.concatenate([weight_of(tap) for tap in range(few)], axis=0),
            jnp.concatenate(moved, axis=0),
            (((0,), (0,)), ((), ())),
            preferred_element_type=jnp.float32,
        )

        @pl.when(part == 0)
        def _():
            for index in range(2 * couples):
                sums[owners + index] = product[index * rows : (index + 1) * rows]

        @pl.when(part > 0)
        def _():
            for index in range(2 * couples):
                sums[owners + index] += product[index * rows : (index + 1) * rows]

        @pl.when(part == parts - 1)
        def _():
            overall = which * pieces + stage
            start_pairs(overall)

            @pl.when(overall >= 1)
            def _():
                finish_pairs(overall - 1)

    @pl.when(step == chunks)
    def _():
        finish_pairs(members * pieces - 1)
        for which in range(members):
            total = paired[which * pairs + me // 2]
            for away in range(1, pairs):
                source = (me // 2 + pairs - away) % pairs
                owner_copy(which, (me // 2 + away) % pairs, source).wait_recv()
                total = total + landed[which * pairs + source]
            out_ref[which] = total
        for which in range(members):
            for away in range(1, pairs):
                owner_copy(which, (me // 2 + away) % pairs, me // 2).wait_send()
            for couple in range(pairs):
                pair_copy(which, couple).wait_send()
        exchange(chunks - 2, few).wait_send()
        exchange(chunks - 1, few).wait_send()


def convolve(mix, x_own, snap_first, snap_second, groups):
    snaps, taps, rows, width = snap_first.shape
    members, tokens = mix.shape[0] // 2, x_own.shape[1]
    span = math.lcm(128, 2 * rows)
    few = 3
    pieces, parts = width // span, taps // few
    couples, pairs = span // (2 * rows), groups // 2
    part = (max(pieces, few), rows, span)
    per = taps + pieces * parts
    sums = (rows, tokens)

    def local(i):
        return jnp.minimum(i, members * per - 1) % per

    def second_block(i):
        at = jnp.maximum(local(i) - taps, 0)
        piece = (lax.axis_index("mp") // (2 * couples) + at // parts + 1) % pieces
        return 0, at % parts, 0, piece

    return pl.pallas_call(
        functools.partial(conv_kernel, taps, groups, span, few, members),
        grid=(members * per + 1,),
        out_shape=jax.ShapeDtypeStruct((members,) + sums, jnp.float32),
        in_specs=[
            pl.BlockSpec(memory_space=pltpu.SMEM),
            pl.BlockSpec((rows, tokens), lambda i: (0, 0)),
            pl.BlockSpec((snaps, 1, rows, width), lambda i: (0, jnp.minimum(local(i), taps - 1), 0, 0)),
            pl.BlockSpec((snaps, few, rows, span), second_block),
        ],
        out_specs=pl.BlockSpec((members,) + sums, lambda i: (0, 0, 0)),
        scratch_shapes=[
            pltpu.VMEM((2,) + part, jnp.float32),
            pltpu.VMEM((2,) + part, jnp.float32),
            pltpu.VMEM((4,) + part, jnp.float32),
            pltpu.VMEM((groups, rows, tokens), jnp.bfloat16),
            pltpu.VMEM((taps, width, tokens), jnp.bfloat16),
            pltpu.VMEM(sums, jnp.float32),
            pltpu.VMEM(sums, jnp.bfloat16),
            pltpu.VMEM((members * groups,) + sums, jnp.float32),
            pltpu.VMEM((members * pairs,) + sums, jnp.float32),
            pltpu.VMEM((members * pairs,) + sums, jnp.float32),
            pltpu.SemaphoreType.DMA((2,)),
            pltpu.SemaphoreType.DMA((4,)),
            pltpu.SemaphoreType.DMA((groups,)),
            pltpu.SemaphoreType.DMA((groups,)),
            pltpu.SemaphoreType.DMA((members * pairs,)),
            pltpu.SemaphoreType.DMA((members * pairs,)),
            pltpu.SemaphoreType.DMA((members * pairs,)),
            pltpu.SemaphoreType.DMA((members * pairs,)),
        ],
        compiler_params=pltpu.CompilerParams(
            collective_id=0,
            has_side_effects=True,
            dimension_semantics=("arbitrary",),
            vmem_limit_bytes=64 * 1024 * 1024 - 65536,
        ),
        name="blend_convolve",
    )(mix, x_own, snap_first, snap_second)


def total_kernel(groups, images, own_ref, out_ref, held, send_sem, recv_sem):
    me = lax.axis_index("mp") * images + lax.axis_index("dp")
    peers = groups * images

    def copy(away):
        to = (me + away) % peers
        return pltpu.make_async_remote_copy(
            src_ref=own_ref,
            dst_ref=held.at[away],
            send_sem=send_sem.at[away],
            recv_sem=recv_sem.at[away],
            device_id={"mp": to // images, "dp": to % images},
            device_id_type=MESH,
        )

    barrier = pltpu.get_barrier_semaphore()
    for away in range(1, peers):
        to = (me + away) % peers
        pl.semaphore_signal(
            barrier,
            inc=1,
            device_id={"mp": to // images, "dp": to % images},
            device_id_type=MESH,
        )
    pl.semaphore_wait(barrier, peers - 1)
    for away in range(1, peers):
        copy(away).start()
    total = own_ref[...]
    for away in range(1, peers):
        copy(away).wait_recv()
        total = total + held[away]
    out_ref[...] = total
    for away in range(1, peers):
        copy(away).wait_send()


def total_over(partial, groups, images):
    peers = groups * images
    return pl.pallas_call(
        functools.partial(total_kernel, groups, images),
        out_shape=jax.ShapeDtypeStruct(partial.shape, jnp.float32),
        in_specs=[pl.BlockSpec(memory_space=pltpu.VMEM)],
        out_specs=pl.BlockSpec(memory_space=pltpu.VMEM),
        scratch_shapes=[
            pltpu.VMEM((peers,) + partial.shape, jnp.float32),
            pltpu.SemaphoreType.DMA((peers,)),
            pltpu.SemaphoreType.DMA((peers,)),
        ],
        compiler_params=pltpu.CompilerParams(collective_id=1, has_side_effects=True),
        name="loss_total",
    )(partial)


def on_device(clean, noise, level_index, snap_first, snap_second, blend, snap_index):
    sigmas = jnp.repeat(noise_scale(level_index), 64)
    spread = sigmas * sigmas + SIGMA_DATA * SIGMA_DATA
    scale_in = 1.0 / jnp.sqrt(spread)
    scale_skip = SIGMA_DATA * SIGMA_DATA / spread
    scale_out = sigmas * SIGMA_DATA / jnp.sqrt(spread)
    weighting = spread / (sigmas * SIGMA_DATA) ** 2
    clean_f = clean.astype(jnp.float32)
    noisy = clean_f + sigmas * noise.astype(jnp.float32)
    x_own = (scale_in * noisy).astype(jnp.bfloat16)
    owned = snap_first.shape[0]
    stored = owned * lax.axis_size("cand")
    groups, images = lax.axis_size("mp"), lax.axis_size("dp")
    onehot = (snap_index[:, :, None] == jnp.arange(stored, dtype=jnp.int32)[None, None, :]).astype(
        jnp.float32
    )
    mixing = jnp.sum(blend[:, :, None] * onehot, 1)
    other_mix = from_partner(mixing, "cand", 0)
    first_slot = lax.axis_index("cand") * owned
    mix = lax.dynamic_slice_in_dim(jnp.concatenate([mixing, other_mix], 0), first_slot, owned, 1)
    members = blend.shape[0]
    features = convolve(mix, x_own, snap_first, snap_second, groups)
    denoised_f = scale_skip[None, None, :] * noisy[None] + scale_out[None, None, :] * features
    partial_value = jnp.sum(
        weighting[None, None, :] * (denoised_f - clean_f[None]) ** 2, axis=(1, 2)
    )
    entries = clean.shape[0] * groups * clean.shape[1] * images
    tile = jnp.broadcast_to(jnp.pad(partial_value, (0, 8 - members))[:, None], (8, 128))
    losses = total_over(tile, groups, images)[:members, 0] / entries
    return (losses, denoised_f.astype(jnp.bfloat16))


def solution(mesh):
    placed = (
        P("mp", "dp"),
        P("mp", "dp"),
        P("dp"),
        P("cand", None, "mp", None),
        P("cand", None, "mp", None),
        P("cand", None),
        P("cand", None),
    )
    return jax.shard_map(
        on_device,
        mesh=mesh,
        in_specs=placed,
        out_specs=(P("cand"), P("cand", "mp", "dp")),
        check_vma=False,
    )
```

```python
import functools
import math

import jax
import jax.numpy as jnp
from jax import lax
from jax.experimental import pallas as pl
from jax.experimental.pallas import tpu as pltpu
from jax.sharding import PartitionSpec as P

LEVELS = 32
SIGMA_DATA = 0.5
MESH = pl.DeviceIdType.MESH


def from_partner(value, axis, apart):
    return lax.ppermute(value, axis, [(i, i ^ 1 << apart) for i in range(lax.axis_size(axis))])


def noise_scale(level_index):
    ratio = 2.0 * level_index.astype(jnp.float32) / (LEVELS - 1) - 1.0
    return jnp.exp(-0.4 + 2.0 * ratio)


def tap_matrix(tap):
    down_by, right_by = tap // 3 - 1, tap % 3 - 1
    source = lax.broadcasted_iota(jnp.int32, (128, 128), 0)
    target = lax.broadcasted_iota(jnp.int32, (128, 128), 1)
    row, col = (target & 63) >> 3, target & 7
    inside = (
        (row + down_by >= 0) & (row + down_by < 8) & (col + right_by >= 0) & (col + right_by < 8)
    )
    hit = (source == target + (down_by * 8 + right_by)) & inside
    return jnp.where(hit, 1.0, 0.0).astype(jnp.bfloat16)


def conv_kernel(
    taps, groups, span, few, mix_ref, x_ref, first_ref, second_ref, out_ref,
    give, mine, got, x_full, x_tap, pre, hidden, sums, paired, leaving, landed,
    send_sem, recv_sem, x_send, x_recv, pair_send, pair_recv, owner_send, owner_recv,
):
    step = pl.program_id(0)
    snaps, rows, width = first_ref.shape[0], first_ref.shape[2], first_ref.shape[3]
    members, tokens = pre.shape[0], pre.shape[2]
    tiles = tokens // 128
    pieces, parts = width // span, taps // few
    chunks = taps + pieces * parts
    pairs, couples = groups // 2, span // (2 * rows)
    cand, me = lax.axis_index("cand"), lax.axis_index("mp")
    partner = 1 - cand
    side = me % 2
    my_piece = me // (2 * couples)
    block = 16 if rows % 16 == 0 else rows

    def exchange(chunk, count):
        return pltpu.make_async_remote_copy(
            src_ref=give.at[chunk % 2, :, pl.ds(0, count)],
            dst_ref=got.at[chunk % 4, :, pl.ds(0, count)],
            send_sem=send_sem.at[chunk % 2],
            recv_sem=recv_sem.at[chunk % 4],
            device_id={"cand": partner},
            device_id_type=MESH,
        )

    def x_copy(away, slot):
        return pltpu.make_async_remote_copy(
            src_ref=x_ref,
            dst_ref=x_full.at[slot],
            send_sem=x_send.at[away],
            recv_sem=x_recv.at[away],
            device_id={"mp": (me + away) % groups},
            device_id_type=MESH,
        )

    def piece_of(stage):
        return (my_piece + stage + 1) % pieces

    def pair_copy(couple):
        return pltpu.make_async_remote_copy(
            src_ref=sums.at[2 * couple + 1 - side],
            dst_ref=paired.at[couple],
            send_sem=pair_send.at[couple],
            recv_sem=pair_recv.at[couple],
            device_id={"mp": me + 1 - 2 * side},
            device_id_type=MESH,
        )

    def owner_copy(couple, slot):
        return pltpu.make_async_remote_copy(
            src_ref=leaving.at[couple],
            dst_ref=landed.at[slot],
            send_sem=owner_send.at[couple],
            recv_sem=owner_recv.at[slot],
            device_id={"mp": 2 * couple + side},
            device_id_type=MESH,
        )

    def start_pairs(stage):
        for which in range(couples):
            pair_copy(piece_of(stage) * couples + which).start()

    def finish_pairs(stage):
        for which in range(couples):
            couple = piece_of(stage) * couples + which
            pair_copy(couple).wait_recv()
            total = paired[couple] + sums[2 * couple + side]
            paired[couple] = total
            leaving[couple] = total.astype(jnp.bfloat16)

            @pl.when(couple != me // 2)
            def _():
                owner_copy(couple, me // 2).start()

    @pl.when(step == 0)
    def _():
        barrier = pltpu.get_barrier_semaphore()
        pl.semaphore_signal(barrier, inc=1, device_id={"cand": partner}, device_id_type=MESH)
        for away in range(1, groups):
            pl.semaphore_signal(
                barrier, inc=1, device_id={"mp": (me + away) % groups}, device_id_type=MESH
            )
        pl.semaphore_wait(barrier, groups)
        for away in range(1, groups):
            x_copy(away, me).start()
        x_full[me] = x_ref[...]
        pre[...] = jnp.zeros_like(pre)

    def blend(source, count, columns, place):
        coeff = [[mix_ref[c, s] for s in range(snaps)] for c in range(2 * members)]
        slot = step % 2

        def body(which, carry):
            at = pl.ds(pl.multiple_of(which * block, block), block)
            for tap in range(count):
                for tile in range(columns // 128):
                    lanes = pl.ds(tile * 128, 128)
                    totals = [None] * (2 * members)
                    for s in range(snaps):
                        value = source[s, tap, at, lanes].astype(jnp.float32)
                        for c in range(2 * members):
                            term = coeff[c][s] * value
                            totals[c] = term if s == 0 else totals[c] + term
                    piece, first = place(tap, tile)
                    for c in range(members):
                        mine[slot, c, piece, at, pl.ds(first, 128)] = totals[c]
                        give[slot, c, piece, at, pl.ds(first, 128)] = totals[members + c]
            return carry

        lax.fori_loop(0, rows // block, body, 0)

    @pl.when((step >= 2) & (step < taps + 2))
    def _():
        exchange(step - 2, pieces).wait_send()

    @pl.when((step >= taps + 2) & (step < chunks))
    def _():
        exchange(step - 2, few).wait_send()

    @pl.when(step < taps)
    def _():
        blend(first_ref, 1, width, lambda tap, tile: (tile * 128 // span, tile * 128 % span))
        exchange(step, pieces).start()

    @pl.when((step >= taps) & (step < chunks))
    def _():
        blend(second_ref, few, span, lambda tap, tile: (tap, tile * 128))
        exchange(step, few).start()

    @pl.when(step == 1)
    def _():
        for away in range(1, groups):
            copy = x_copy(away, (me + groups - away) % groups)
            copy.wait_send()
            copy.wait_recv()

    done = step - 1

    def weight_of(c, piece):
        return (mine[done % 2, c, piece] + got[done % 4, c, piece]).astype(jnp.bfloat16)

    @pl.when((step >= 1) & (done < taps))
    def _():
        shift = tap_matrix(done)
        for group in range(groups):
            for tile in range(tiles):
                lanes = pl.ds(tile * 128, 128)
                x_tap[pl.ds(group * rows, rows), lanes] = jnp.dot(
                    x_full[group, :, lanes], shift, preferred_element_type=jnp.float32
                ).astype(jnp.bfloat16)
        exchange(done, pieces).wait_recv()
        for c in range(members):
            weight = jnp.concatenate([weight_of(c, piece) for piece in range(pieces)], axis=1)
            pre[c] += jnp.dot(weight, x_tap[...], preferred_element_type=jnp.float32)

    @pl.when(done == taps - 1)
    def _():
        value = pre[...]
        hidden[...] = (value * jax.nn.sigmoid(value)).astype(jnp.bfloat16)

    @pl.when((step >= 1) & (done >= taps))
    def _():
        at = done - taps
        stage, part = at // parts, at % parts
        owners = piece_of(stage) * 2 * couples
        shifts = [tap_matrix(part * few + tap) for tap in range(few)]
        exchange(done, few).wait_recv()
        for c in range(members):
            moved = [
                jnp.concatenate(
                    [
                        jnp.dot(
                            hidden[c, :, pl.ds(tile * 128, 128)],
                            shift,
                            preferred_element_type=jnp.float32,
                        ).astype(jnp.bfloat16)
                        for tile in range(tiles)
                    ],
                    axis=1,
                )
                for shift in shifts
            ]
            weight = jnp.concatenate([weight_of(c, tap) for tap in range(few)], axis=0)
            product = lax.dot_general(
                weight,
                jnp.concatenate(moved, axis=0),
                (((0,), (0,)), ((), ())),
                preferred_element_type=jnp.float32,
            )
            lanes = pl.ds(c * tokens, tokens)

            @pl.when(part == 0)
            def _():
                for which in range(2 * couples):
                    sums[owners + which, :, lanes] = product[which * rows : (which + 1) * rows]

            @pl.when(part > 0)
            def _():
                for which in range(2 * couples):
                    sums[owners + which, :, lanes] += product[which * rows : (which + 1) * rows]

        @pl.when(part == parts - 1)
        def _():
            start_pairs(stage)

            @pl.when(stage >= 1)
            def _():
                finish_pairs(stage - 1)

    @pl.when(step == chunks)
    def _():
        finish_pairs(pieces - 1)
        total = paired[me // 2]
        for away in range(1, pairs):
            source = (me // 2 + pairs - away) % pairs
            owner_copy((me // 2 + away) % pairs, source).wait_recv()
            total = total + landed[source].astype(jnp.float32)
        out_ref[...] = total
        for away in range(1, pairs):
            owner_copy((me // 2 + away) % pairs, me // 2).wait_send()
        for couple in range(pairs):
            pair_copy(couple).wait_send()
        exchange(chunks - 2, few).wait_send()
        exchange(chunks - 1, few).wait_send()


def convolve(mix, x_own, snap_first, snap_second, groups):
    snaps, taps, rows, width = snap_first.shape
    members, tokens = mix.shape[0] // 2, x_own.shape[1]
    span = math.lcm(128, 2 * rows)
    few = 3
    pieces, parts = width // span, taps // few
    couples, pairs = span // (2 * rows), groups // 2
    part = (members, max(pieces, few), rows, span)
    sums = (rows, members * tokens)

    def second_block(i):
        at = jnp.clip(i - taps, 0, pieces * parts - 1)
        piece = (lax.axis_index("mp") // (2 * couples) + at // parts + 1) % pieces
        return 0, at % parts, 0, piece

    return pl.pallas_call(
        functools.partial(conv_kernel, taps, groups, span, few),
        grid=(taps + pieces * parts + 1,),
        out_shape=jax.ShapeDtypeStruct(sums, jnp.float32),
        in_specs=[
            pl.BlockSpec(memory_space=pltpu.SMEM),
            pl.BlockSpec((rows, tokens), lambda i: (0, 0)),
            pl.BlockSpec((snaps, 1, rows, width), lambda i: (0, jnp.minimum(i, taps - 1), 0, 0)),
            pl.BlockSpec((snaps, few, rows, span), second_block),
        ],
        out_specs=pl.BlockSpec(sums, lambda i: (0, 0)),
        scratch_shapes=[
            pltpu.VMEM((2,) + part, jnp.float32),
            pltpu.VMEM((2,) + part, jnp.float32),
            pltpu.VMEM((4,) + part, jnp.float32),
            pltpu.VMEM((groups, rows, tokens), jnp.bfloat16),
            pltpu.VMEM((width, tokens), jnp.bfloat16),
            pltpu.VMEM((members, rows, tokens), jnp.float32),
            pltpu.VMEM((members, rows, tokens), jnp.bfloat16),
            pltpu.VMEM((groups,) + sums, jnp.float32),
            pltpu.VMEM((pairs,) + sums, jnp.float32),
            pltpu.VMEM((pairs,) + sums, jnp.bfloat16),
            pltpu.VMEM((pairs,) + sums, jnp.bfloat16),
            pltpu.SemaphoreType.DMA((2,)),
            pltpu.SemaphoreType.DMA((4,)),
            pltpu.SemaphoreType.DMA((groups,)),
            pltpu.SemaphoreType.DMA((groups,)),
            pltpu.SemaphoreType.DMA((pairs,)),
            pltpu.SemaphoreType.DMA((pairs,)),
            pltpu.SemaphoreType.DMA((pairs,)),
            pltpu.SemaphoreType.DMA((pairs,)),
        ],
        compiler_params=pltpu.CompilerParams(
            collective_id=0,
            has_side_effects=True,
            dimension_semantics=("arbitrary",),
            vmem_limit_bytes=64 * 1024 * 1024 - 65536,
        ),
        name="blend_convolve",
    )(mix, x_own, snap_first, snap_second)


def total_kernel(groups, images, own_ref, out_ref, held, send_sem, recv_sem):
    me = lax.axis_index("mp") * images + lax.axis_index("dp")
    peers = groups * images

    def copy(away):
        to = (me + away) % peers
        return pltpu.make_async_remote_copy(
            src_ref=own_ref,
            dst_ref=held.at[away],
            send_sem=send_sem.at[away],
            recv_sem=recv_sem.at[away],
            device_id={"mp": to // images, "dp": to % images},
            device_id_type=MESH,
        )

    barrier = pltpu.get_barrier_semaphore()
    for away in range(1, peers):
        to = (me + away) % peers
        pl.semaphore_signal(
            barrier,
            inc=1,
            device_id={"mp": to // images, "dp": to % images},
            device_id_type=MESH,
        )
    pl.semaphore_wait(barrier, peers - 1)
    for away in range(1, peers):
        copy(away).start()
    total = own_ref[...]
    for away in range(1, peers):
        copy(away).wait_recv()
        total = total + held[away]
    out_ref[...] = total
    for away in range(1, peers):
        copy(away).wait_send()


def total_over(partial, groups, images):
    peers = groups * images
    return pl.pallas_call(
        functools.partial(total_kernel, groups, images),
        out_shape=jax.ShapeDtypeStruct(partial.shape, jnp.float32),
        in_specs=[pl.BlockSpec(memory_space=pltpu.VMEM)],
        out_specs=pl.BlockSpec(memory_space=pltpu.VMEM),
        scratch_shapes=[
            pltpu.VMEM((peers,) + partial.shape, jnp.float32),
            pltpu.SemaphoreType.DMA((peers,)),
            pltpu.SemaphoreType.DMA((peers,)),
        ],
        compiler_params=pltpu.CompilerParams(collective_id=1, has_side_effects=True),
        name="loss_total",
    )(partial)


def on_device(clean, noise, level_index, snap_first, snap_second, blend, snap_index):
    sigmas = jnp.repeat(noise_scale(level_index), 64)
    spread = sigmas * sigmas + SIGMA_DATA * SIGMA_DATA
    scale_in = 1.0 / jnp.sqrt(spread)
    scale_skip = SIGMA_DATA * SIGMA_DATA / spread
    scale_out = sigmas * SIGMA_DATA / jnp.sqrt(spread)
    weighting = spread / (sigmas * SIGMA_DATA) ** 2
    clean_f = clean.astype(jnp.float32)
    noisy = clean_f + sigmas * noise.astype(jnp.float32)
    x_own = (scale_in * noisy).astype(jnp.bfloat16)
    owned = snap_first.shape[0]
    stored = owned * lax.axis_size("cand")
    groups, images = lax.axis_size("mp"), lax.axis_size("dp")
    onehot = (snap_index[:, :, None] == jnp.arange(stored, dtype=jnp.int32)[None, None, :]).astype(
        jnp.float32
    )
    mixing = jnp.sum(blend[:, :, None] * onehot, 1)
    other_mix = from_partner(mixing, "cand", 0)
    first_slot = lax.axis_index("cand") * owned
    mix = lax.dynamic_slice_in_dim(jnp.concatenate([mixing, other_mix], 0), first_slot, owned, 1)
    members = blend.shape[0]
    feature = convolve(mix, x_own, snap_first, snap_second, groups)
    tokens = clean.shape[1]
    features = jnp.stack([feature[:, c * tokens : (c + 1) * tokens] for c in range(members)], 0)
    denoised_f = scale_skip[None, None, :] * noisy[None] + scale_out[None, None, :] * features
    partial_value = jnp.sum(
        weighting[None, None, :] * (denoised_f - clean_f[None]) ** 2, axis=(1, 2)
    )
    entries = clean.shape[0] * groups * clean.shape[1] * images
    tile = jnp.broadcast_to(jnp.pad(partial_value, (0, 8 - members))[:, None], (8, 128))
    losses = total_over(tile, groups, images)[:members, 0] / entries
    return (losses, denoised_f.astype(jnp.bfloat16))


def solution(mesh):
    placed = (
        P("mp", "dp"),
        P("mp", "dp"),
        P("dp"),
        P("cand", None, "mp", None),
        P("cand", None, "mp", None),
        P("cand", None),
        P("cand", None),
    )
    return jax.shard_map(
        on_device,
        mesh=mesh,
        in_specs=placed,
        out_specs=(P("cand"), P("cand", "mp", "dp")),
        check_vma=False,
    )
```
